32 devices in a mesh: prow: 4 (over y, x), pcol: 8 (over z, core).
Axes of the slice: x: 2, y: 2, z: 4, core: 2. Of those that a mesh axis runs over, the one named last changes fastest.
Arguments:
- ancestor: float32 [12288, 12288], P('prow', 'pcol'), may hold values from -448 to 15360, as said below
- factor: bfloat16 [2, 12288, 256], P(None, 'prow'), may hold values from -0.0009765625 to 0.0009765625
- inverse_diag: bfloat16 [2, 256, 256], replicated, may hold values from -6 to 6
- block_mask: int32 [2, 48], replicated, may hold values 0 or 1
Outputs:
- column_block: float32 [2, 12288, 256], P(None, ('prow', 'pcol'))
- diagonal: float32 [2, 256, 256], replicated
The draws below stay inside these ranges and needn't reach their ends.
Inputs may be any that keep to these rules, and one draw needn't show every extreme that they name: `ancestor`: symmetric.
All inputs are finite; a program needn't handle non-finite values.
Results may differ from the reference program's by a relative error of at most 0.0003.
Values may be sent and summed in bfloat16 or wider, within the bound.
A program may use at most 64 MiB of HBM per device.

```python
import math
import jax
import jax.numpy as jnp
from jax import lax

WIDTH = 256
NB = 48
SN = 2
ORDER = 12288


def draw_ancestor(key, part):
    order = NB * WIDTH
    first_key = jax.random.fold_in(jax.random.fold_in(key, 17), 0)
    noise = jnp.clip(jax.random.normal(first_key, (order, order), jnp.float32), -4.0, 4.0)
    base = (noise + noise.T) * (0.5 * order / (3.0 * math.sqrt(2.0 * order)))
    base = base + jnp.diag(jnp.full((order,), 0.5 * order, jnp.float32))
    return base


def with_ends(entries, own_key, low, high):
    shape = entries.shape
    index_at = [jax.random.randint(jax.random.fold_in(own_key, axis), (), 0, shape[axis]) for axis in range(len(shape))]
    entries = entries.at[tuple(index_at)].set(low)
    longest = shape.index(max(shape))
    index_at[longest] = (index_at[longest] + 1) % shape[longest]
    return entries.at[tuple(index_at)].set(high)


def levels(rng, shape, pieces, least, high):
    factor_of, own = 1.0, jax.random.fold_in(rng, 6)
    for dim, parts in pieces:
        steps = jnp.exp(jax.random.uniform(jax.random.fold_in(own, dim), (parts,), jnp.float32, least / len(pieces), high / len(pieces)))
        factor_of = factor_of * jnp.repeat(steps, shape[dim] // parts).reshape([-1 if axis == dim else 1 for axis in range(len(shape))])
    return factor_of


def scatter_about(own_key, extent, width, limit, cuts=(), dtype=jnp.bfloat16):
    values = width * jax.random.normal(own_key, extent, jnp.float32)
    if cuts:
        values = values * levels(own_key, extent, cuts, -0.22, 0.18)
    return jnp.clip(values, -limit, limit).astype(dtype)


def setup_inputs(seed: int = 0) -> dict:
    seeds = jax.random.split(jax.random.key(seed), 5)
    ancestor = draw_ancestor(jax.random.fold_in(seeds[4], 71), 0)
    factor = scatter_about(seeds[1], (SN, ORDER, WIDTH), (2.0 / ORDER), 0.0009765625, ((1, 4),))
    inverse_diag = scatter_about(seeds[2], (SN, WIDTH, WIDTH), 1.0, 6.0)
    block_mask = with_ends((jax.random.randint(seeds[3], (SN, NB), 0, 2) < 1).astype(jnp.int32), jax.random.fold_in(seeds[3], 1), 0, 1)
    return dict(ancestor=ancestor, factor=factor, inverse_diag=inverse_diag, block_mask=block_mask)


def reference(ancestor, factor, inverse_diag, block_mask):
    row_mask = jnp.repeat(block_mask, WIDTH, axis=1).astype(jnp.float32)
    blocks = []
    diagonals = []
    for supernode in range(SN):
        masked = factor[supernode].astype(jnp.float32) * row_mask[supernode][:, None]
        product = jnp.dot(ancestor, masked, precision=lax.Precision.HIGHEST, preferred_element_type=jnp.float32)
        column = -row_mask[supernode][:, None] * product
        inner = jnp.dot(masked.T, column, precision=lax.Precision.HIGHEST, preferred_element_type=jnp.float32)
        blocks.append(column)
        diagonals.append(inverse_diag[supernode].astype(jnp.float32) - inner)
    return jnp.stack(blocks, 0), jnp.stack(diagonals, 0)
```

```python
import jax
import jax.numpy as jnp
from jax import lax
from jax.sharding import PartitionSpec as P

WIDTH = 256


def split(x):
    high = lax.reduce_precision(x, 8, 7)
    low = x - high
    return high.astype(jnp.bfloat16), low.astype(jnp.bfloat16)


def dot(a, b):
    return jnp.dot(a, b, preferred_element_type=jnp.float32)


def shards(ancestor, factor, inverse_diag, block_mask):
    rows_here = ancestor.shape[0]
    count, _, width = factor.shape
    n_rows = lax.axis_size("prow")
    n_cols = lax.axis_size("pcol")
    column = lax.axis_index("pcol")
    grid_row = lax.axis_index("prow")
    slab = rows_here // n_cols
    row_mask = jnp.repeat(block_mask, WIDTH, axis=1).astype(jnp.float32)
    own_mask = lax.dynamic_slice_in_dim(row_mask, grid_row * rows_here, rows_here, 1)
    masked = factor * own_mask[:, :, None].astype(factor.dtype)
    turned = masked.transpose(0, 2, 1).reshape(count * width, rows_here)
    high, low = split(ancestor)
    partial = dot(turned, high) + dot(turned, low)
    summed = lax.psum_scatter(partial, "prow", scatter_dimension=1, tiled=True)
    pairs = [(r * n_cols + c, c * n_rows + r) for r in range(n_rows) for c in range(n_cols)]
    placed = lax.ppermute(summed, ("prow", "pcol"), pairs)
    slab_mask = lax.dynamic_slice_in_dim(own_mask, column * slab, slab, 1)
    placed = placed.reshape(count, width, slab)
    column_block = -slab_mask[:, :, None] * placed.transpose(0, 2, 1)
    own_slab = lax.dynamic_slice_in_dim(masked, column * slab, slab, 1)
    high, low = split(column_block)
    term = jnp.stack([dot(own_slab[k].T, high[k]) + dot(own_slab[k].T, low[k]) for k in range(count)])
    total = lax.psum(term, ("prow", "pcol"))
    diagonal = inverse_diag.astype(jnp.float32) - total
    return (column_block, diagonal)


def solution(mesh):
    return jax.shard_map(
        shards,
        mesh=mesh,
        in_specs=(P("prow", "pcol"), P(None, "prow", None), P(), P()),
        out_specs=(P(None, ("prow", "pcol"), None), P()),
        check_vma=False,
    )
```

```python
import jax
import jax.numpy as jnp
from jax import lax
from jax.experimental import pallas as pl
from jax.experimental.pallas import tpu as pltpu
from jax.sharding import PartitionSpec as P

WIDTH = 256


def split(x):
    high = lax.reduce_precision(x, 8, 7)
    low = x - high
    return high.astype(jnp.bfloat16), low.astype(jnp.bfloat16)


def dot(a, b):
    return jnp.dot(a, b, preferred_element_type=jnp.float32)


MESH = pl.DeviceIdType.MESH


def levels():
    n_rows = lax.axis_size("prow")
    n_deep = lax.axis_size("pcol") // 2
    row = lax.axis_index("prow")
    column = lax.axis_index("pcol")
    deep, core = lax.div(column, 2), lax.rem(column, 2)
    return (
        (2, core, lambda p: (row, deep * 2 + p)),
        (n_rows, row, lambda p: (p, column)),
        (n_deep, deep, lambda p: (row, p * 2 + core)),
    )


def greet(peers):
    barrier = pltpu.get_barrier_semaphore()
    for peer in peers:
        pl.semaphore_signal(barrier, inc=1, device_id=peer, device_id_type=MESH)
    pl.semaphore_wait(barrier, len(peers))


def part(ref, start, size):
    return ref.at[pl.ds(pl.multiple_of(start, 8), size)]


def sum_everywhere(term, acc, landed, gathered, sems):
    height = term.shape[0]
    start = 0
    size = height
    source = term
    sent = []
    starts = []
    number = 0
    slot = 0
    for n, mine, device in levels():
        size = size // n
        copies = []
        for d in range(1, n):
            peer = lax.rem(mine + d, n)
            copy = pltpu.make_async_remote_copy(
                part(source, start + peer * size, size),
                landed.at[pl.ds(slot + (d - 1) * size, size)],
                sems.at[0, number],
                sems.at[1, number],
                device_id=device(peer),
                device_id_type=MESH,
            )
            copy.start()
            copies.append(copy)
            number += 1
        start = start + mine * size
        starts.append((start, size))
        total = part(source, start, size)[...]
        for d in range(1, n):
            copies[d - 1].wait_recv()
            total = total + landed[pl.ds(slot + (d - 1) * size, size)]
        slot += (n - 1) * size
        part(acc, start, size)[...] = total
        source = acc
        sent += copies
    part(gathered, start, size)[...] = total
    for (n, mine, device), (start, size) in reversed(list(zip(levels(), starts))):
        copies = []
        for d in range(1, n):
            peer = lax.rem(mine + d, n)
            copy = pltpu.make_async_remote_copy(
                part(gathered, start, size),
                part(gathered, start, size),
                sems.at[0, number],
                sems.at[1, number],
                device_id=device(peer),
                device_id_type=MESH,
            )
            copy.start()
            copies.append(copy)
            number += 1
        for copy in copies:
            copy.wait_recv()
        sent += copies
    for copy in sent:
        copy.wait_send()


def diagonal_kernel(term, inverse, out, acc, landed, gathered, sems):
    greet([device(lax.rem(mine + d, n)) for n, mine, device in levels() for d in range(1, n)])
    sum_everywhere(term, acc, landed, gathered, sems)
    out[...] = inverse[...].astype(jnp.float32) - gathered[...]


def finish(term, inverse):
    height, width = term.shape
    sizes = [2, lax.axis_size("prow"), lax.axis_size("pcol") // 2]
    copies = sum(n - 1 for n in sizes) * 2
    block = pltpu.VMEM((height, width), jnp.float32)
    vmem = pl.BlockSpec(memory_space=pltpu.VMEM)
    return pl.pallas_call(
        diagonal_kernel,
        out_shape=jax.ShapeDtypeStruct((height, width), jnp.float32),
        in_specs=[vmem, vmem],
        out_specs=vmem,
        scratch_shapes=[block, block, block, pltpu.SemaphoreType.DMA((2, copies))],
        compiler_params=pltpu.CompilerParams(collective_id=0, has_side_effects=True),
    )(term, inverse)


def shards(ancestor, factor, inverse_diag, block_mask):
    rows_here = ancestor.shape[0]
    count, _, width = factor.shape
    n_rows = lax.axis_size("prow")
    n_cols = lax.axis_size("pcol")
    column = lax.axis_index("pcol")
    grid_row = lax.axis_index("prow")
    slab = rows_here // n_cols
    row_mask = jnp.repeat(block_mask, WIDTH, axis=1).astype(jnp.float32)
    own_mask = lax.dynamic_slice_in_dim(row_mask, grid_row * rows_here, rows_here, 1)
    masked = factor * own_mask[:, :, None].astype(factor.dtype)
    turned = masked.transpose(0, 2, 1).reshape(count * width, rows_here)
    high, low = split(ancestor)
    partial = dot(turned, high) + dot(turned, low)
    summed = lax.psum_scatter(partial, "prow", scatter_dimension=1, tiled=True)
    pairs = [(r * n_cols + c, c * n_rows + r) for r in range(n_rows) for c in range(n_cols)]
    placed = lax.ppermute(summed, ("prow", "pcol"), pairs)
    slab_mask = lax.dynamic_slice_in_dim(own_mask, column * slab, slab, 1)
    placed = placed.reshape(count, width, slab)
    column_block = -slab_mask[:, :, None] * placed.transpose(0, 2, 1)
    own_slab = lax.dynamic_slice_in_dim(masked, column * slab, slab, 1)
    high, low = split(column_block)
    term = jnp.stack([dot(own_slab[k].T, high[k]) + dot(own_slab[k].T, low[k]) for k in range(count)])
    devices = n_rows * n_cols
    if n_cols % 2 or (count * width) % (8 * devices):
        total = lax.psum(term, ("prow", "pcol"))
        return (column_block, inverse_diag.astype(jnp.float32) - total)
    flat = (count * width, width)
    diagonal = finish(term.reshape(flat), inverse_diag.reshape(flat))
    return (column_block, diagonal.reshape(inverse_diag.shape))


def solution(mesh):
    return jax.shard_map(
        shards,
        mesh=mesh,
        in_specs=(P("prow", "pcol"), P(None, "prow", None), P(), P()),
        out_specs=(P(None, ("prow", "pcol"), None), P()),
        check_vma=False,
    )
```

```python
import jax
import jax.numpy as jnp
from jax import lax
from jax.experimental import pallas as pl
from jax.experimental.pallas import tpu as pltpu
from jax.sharding import PartitionSpec as P

WIDTH = 256


def split(x):
    high = lax.reduce_precision(x, 8, 7)
    low = x - high
    return high.astype(jnp.bfloat16), low.astype(jnp.bfloat16)


def dot(a, b):
    return jnp.dot(a, b, preferred_element_type=jnp.float32)


MESH = pl.DeviceIdType.MESH


def levels():
    n_rows = lax.axis_size("prow")
    n_deep = lax.axis_size("pcol") // 2
    row = lax.axis_index("prow")
    column = lax.axis_index("pcol")
    deep, core = lax.div(column, 2), lax.rem(column, 2)
    return (
        (2, core, lambda p: (row, deep * 2 + p)),
        (n_rows, row, lambda p: (p, column)),
        (n_deep, deep, lambda p: (row, p * 2 + core)),
    )


def greet(peers):
    barrier = pltpu.get_barrier_semaphore()
    for peer in peers:
        pl.semaphore_signal(barrier, inc=1, device_id=peer, device_id_type=MESH)
    pl.semaphore_wait(barrier, len(peers))


def part(ref, start, size):
    return ref.at[pl.ds(pl.multiple_of(start, 8), size)]


def sum_everywhere(term, acc, landed, gathered, sems):
    height = term.shape[0]
    start = 0
    size = height
    source = term
    sent = []
    starts = []
    number = 0
    slot = 0
    for n, mine, device in levels():
        size = size // n
        copies = []
        for d in range(1, n):
            peer = lax.rem(mine + d, n)
            copy = pltpu.make_async_remote_copy(
                part(source, start + peer * size, size),
                landed.at[pl.ds(slot + (d - 1) * size, size)],
                sems.at[0, number],
                sems.at[1, number],
                device_id=device(peer),
                device_id_type=MESH,
            )
            copy.start()
            copies.append(copy)
            number += 1
        start = start + mine * size
        starts.append((start, size))
        total = part(source, start, size)[...]
        for d in range(1, n):
            copies[d - 1].wait_recv()
            total = total + landed[pl.ds(slot + (d - 1) * size, size)]
        slot += (n - 1) * size
        part(acc, start, size)[...] = total
        source = acc
        sent += copies
    part(gathered, start, size)[...] = total
    for (n, mine, device), (start, size) in reversed(list(zip(levels(), starts))):
        copies = []
        for d in range(1, n):
            peer = lax.rem(mine + d, n)
            copy = pltpu.make_async_remote_copy(
                part(gathered, start, size),
                part(gathered, start, size),
                sems.at[0, number],
                sems.at[1, number],
                device_id=device(peer),
                device_id_type=MESH,
            )
            copy.start()
            copies.append(copy)
            number += 1
        for copy in copies:
            copy.wait_recv()
        sent += copies
    for copy in sent:
        copy.wait_send()


def diagonal_kernel(term, inverse, out, acc, landed, gathered, sems):
    greet([device(lax.rem(mine + d, n)) for n, mine, device in levels() for d in range(1, n)])
    sum_everywhere(term, acc, landed, gathered, sems)
    out[...] = inverse[...].astype(jnp.float32) - gathered[...]


def finish(term, inverse):
    height, width = term.shape
    sizes = [2, lax.axis_size("prow"), lax.axis_size("pcol") // 2]
    copies = sum(n - 1 for n in sizes) * 2
    block = pltpu.VMEM((height, width), jnp.float32)
    vmem = pl.BlockSpec(memory_space=pltpu.VMEM)
    return pl.pallas_call(
        diagonal_kernel,
        out_shape=jax.ShapeDtypeStruct((height, width), jnp.float32),
        in_specs=[vmem, vmem],
        out_specs=vmem,
        scratch_shapes=[block, block, block, pltpu.SemaphoreType.DMA((2, copies))],
        compiler_params=pltpu.CompilerParams(collective_id=0, has_side_effects=True),
    )(term, inverse)


LANES = 128


def remote(source, target, sems, piece, number, device):
    return pltpu.make_async_remote_copy(
        source,
        target,
        sems.at[0, piece, number],
        sems.at[1, piece, number],
        device_id=device,
        device_id_type=MESH,
    )


def product_kernel(turned, ancestor, out, tiles, parts, first, second, sums, ended, landing, loads, sems):
    n_rows = lax.axis_size("prow")
    n_cols = lax.axis_size("pcol")
    row = lax.axis_index("prow")
    column = lax.axis_index("pcol")
    slab = out.shape[1]
    pieces = slab // LANES
    half = out.shape[0] // 2
    flip_x = row + 1 - 2 * lax.rem(row, 2)
    flip_y = lax.rem(row + 2, 4)
    flip_both = 3 - row
    x_peer, y_peer = (flip_x, column), (flip_y, column)
    place = column * n_rows + row
    target = (lax.div(place, n_cols), lax.rem(place, n_cols))
    here = row * n_cols + column
    origin = (lax.rem(here, n_rows), lax.div(here, n_rows))
    order = (flip_both, flip_x, flip_y, row)
    buffers = tiles.shape[0]
    upper, lower = pl.ds(0, half), pl.ds(half, half)

    def load(t):
        start = pl.multiple_of(order[t % 4] * slab + (t // 4) * LANES, LANES)
        return pltpu.make_async_copy(ancestor.at[:, pl.ds(start, LANES)], tiles.at[t % buffers], loads.at[t])

    for t in range(buffers):
        load(t).start()

    barrier = pltpu.get_barrier_semaphore()
    pl.semaphore_signal(barrier, inc=1, device_id=x_peer, device_id_type=MESH)
    pl.semaphore_signal(barrier, inc=1, device_id=y_peer, device_id_type=MESH)

    @pl.when(place != here)
    def _():
        pl.semaphore_signal(barrier, inc=1, device_id=origin, device_id_type=MESH)
        pl.semaphore_wait(barrier, 3)

    @pl.when(place == here)
    def _():
        pl.semaphore_wait(barrier, 2)

    def early(j):
        return (
            remote(parts.at[4 * j, upper], first.at[j, 0], sems, j, 0, x_peer),
            remote(parts.at[4 * j + 1, upper], first.at[j, 1], sems, j, 1, x_peer),
            remote(parts.at[4 * j, lower], first.at[j, 2], sems, j, 2, y_peer),
            remote(parts.at[4 * j + 2, lower], first.at[j, 3], sems, j, 3, y_peer),
        )

    def late(j):
        return (
            remote(sums.at[j, 0], second.at[j, 0], sems, j, 4, y_peer),
            remote(sums.at[j, 1], second.at[j, 1], sems, j, 5, x_peer),
        )

    def final(j):
        return remote(ended.at[j], landing.at[j], sems, j, 6, target)

    def compute(j):
        for q in range(4):
            t = 4 * j + q
            load(t).wait()
            value = tiles[t % buffers]
            high = value.astype(jnp.bfloat16)
            low = (value - high.astype(jnp.float32)).astype(jnp.bfloat16)
            both = dot(turned[...], jnp.concatenate([high, low], axis=1))
            parts[t] = both[:, :LANES] + both[:, LANES:]
            if t + buffers < 4 * pieces:
                load(t + buffers).start()
            copies = early(j)
            for i in ((0, 2), (1,), (3,), ())[q]:
                copies[i].start()

    def forward(j):
        copies = early(j)
        copies[0].wait_recv()
        sums[j, 0] = parts[4 * j + 2, upper] + first[j, 0]
        late(j)[0].start()
        copies[2].wait_recv()
        sums[j, 1] = parts[4 * j + 1, lower] + first[j, 2]
        late(j)[1].start()

    def end(j):
        copies = early(j)
        copies[1].wait_recv()
        copies[3].wait_recv()
        late(j)[0].wait_recv()
        late(j)[1].wait_recv()
        ended[j, upper] = parts[4 * j + 3, upper] + first[j, 1] + second[j, 0]
        ended[j, lower] = parts[4 * j + 3, lower] + first[j, 3] + second[j, 1]

        @pl.when(place != here)
        def _():
            final(j).start()

    for j in range(pieces):
        compute(j)
        if j >= 1:
            forward(j - 1)
        if j >= 2:
            end(j - 2)
    forward(pieces - 1)
    for j in range(max(pieces - 2, 0), pieces):
        end(j)
    for j in range(pieces):
        lanes = pl.ds(j * LANES, LANES)

        @pl.when(place != here)
        def _():
            final(j).wait_recv()
            out[:, lanes] = landing[j]
            final(j).wait_send()

        @pl.when(place == here)
        def _():
            out[:, lanes] = ended[j]

        for copy in early(j) + late(j):
            copy.wait_send()


def product(turned, ancestor):
    height, depth = turned.shape
    slab = ancestor.shape[1] // lax.axis_size("prow")
    pieces = slab // LANES
    half = height // 2
    vmem = pl.BlockSpec(memory_space=pltpu.VMEM)
    f32 = jnp.float32
    return pl.pallas_call(
        product_kernel,
        out_shape=jax.ShapeDtypeStruct((height, slab), f32),
        in_specs=[vmem, pl.BlockSpec(memory_space=pl.ANY)],
        out_specs=vmem,
        scratch_shapes=[
            pltpu.VMEM((4, depth, LANES), f32),
            pltpu.VMEM((4 * pieces, height, LANES), f32),
            pltpu.VMEM((pieces, 4, half, LANES), f32),
            pltpu.VMEM((pieces, 2, half, LANES), f32),
            pltpu.VMEM((pieces, 2, half, LANES), f32),
            pltpu.VMEM((pieces, height, LANES), f32),
            pltpu.VMEM((pieces, height, LANES), f32),
            pltpu.SemaphoreType.DMA((4 * pieces,)),
            pltpu.SemaphoreType.DMA((2, pieces, 7)),
        ],
        compiler_params=pltpu.CompilerParams(
            collective_id=1, has_side_effects=True, vmem_limit_bytes=48 * 1024 * 1024
        ),
    )(turned, ancestor)


def product_plain(turned, ancestor):
    n_rows = lax.axis_size("prow")
    n_cols = lax.axis_size("pcol")
    high, low = split(ancestor)
    partial = dot(turned, high) + dot(turned, low)
    summed = lax.psum_scatter(partial, "prow", scatter_dimension=1, tiled=True)
    pairs = [(r * n_cols + c, c * n_rows + r) for r in range(n_rows) for c in range(n_cols)]
    return lax.ppermute(summed, ("prow", "pcol"), pairs)


def shards(ancestor, factor, inverse_diag, block_mask):
    rows_here = ancestor.shape[0]
    count, _, width = factor.shape
    n_rows = lax.axis_size("prow")
    n_cols = lax.axis_size("pcol")
    column = lax.axis_index("pcol")
    grid_row = lax.axis_index("prow")
    slab = rows_here // n_cols
    row_mask = jnp.repeat(block_mask, WIDTH, axis=1).astype(jnp.float32)
    own_mask = lax.dynamic_slice_in_dim(row_mask, grid_row * rows_here, rows_here, 1)
    masked = factor * own_mask[:, :, None].astype(factor.dtype)
    turned = masked.transpose(0, 2, 1).reshape(count * width, rows_here)
    fits = n_rows == 4 and count % 2 == 0 and slab % LANES == 0
    placed = (product if fits else product_plain)(turned, ancestor)
    slab_mask = lax.dynamic_slice_in_dim(own_mask, column * slab, slab, 1)
    placed = placed.reshape(count, width, slab)
    column_block = -slab_mask[:, :, None] * placed.transpose(0, 2, 1)
    own_slab = lax.dynamic_slice_in_dim(masked, column * slab, slab, 1)
    high, low = split(column_block)
    term = jnp.stack([dot(own_slab[k].T, high[k]) + dot(own_slab[k].T, low[k]) for k in range(count)])
    devices = n_rows * n_cols
    if n_cols % 2 or (count * width) % (8 * devices):
        total = lax.psum(term, ("prow", "pcol"))
        return (column_block, inverse_diag.astype(jnp.float32) - total)
    flat = (count * width, width)
    diagonal = finish(term.reshape(flat), inverse_diag.reshape(flat))
    return (column_block, diagonal.reshape(inverse_diag.shape))


def solution(mesh):
    return jax.shard_map(
        shards,
        mesh=mesh,
        in_specs=(P("prow", "pcol"), P(None, "prow", None), P(), P()),
        out_specs=(P(None, ("prow", "pcol"), None), P()),
        check_vma=False,
    )
```

```python
import jax
import jax.numpy as jnp
from jax import lax
from jax.experimental import pallas as pl
from jax.experimental.pallas import tpu as pltpu
from jax.sharding import PartitionSpec as P

WIDTH = 256


def split(x):
    high = lax.reduce_precision(x, 8, 7)
    low = x - high
    return high.astype(jnp.bfloat16), low.astype(jnp.bfloat16)


def dot(a, b):
    return jnp.dot(a, b, preferred_element_type=jnp.float32)


MESH = pl.DeviceIdType.MESH


def levels():
    n_rows = lax.axis_size("prow")
    n_deep = lax.axis_size("pcol") // 2
    row = lax.axis_index("prow")
    column = lax.axis_index("pcol")
    deep, core = lax.div(column, 2), lax.rem(column, 2)
    return (
        (2, core, lambda p: (row, deep * 2 + p)),
        (n_rows, row, lambda p: (p, column)),
        (n_deep, deep, lambda p: (row, p * 2 + core)),
    )


def part(ref, start, size):
    return ref.at[pl.ds(pl.multiple_of(start, 8), size)]


def sum_everywhere(term, acc, landed, gathered, sems, meanwhile):
    height = term.shape[0]
    start = 0
    size = height
    source = term
    sent = []
    starts = []
    number = 0
    slot = 0
    for depth, (n, mine, device) in enumerate(levels()):
        size = size // n
        copies = []
        for d in range(1, n):
            peer = lax.rem(mine + d, n)
            copy = pltpu.make_async_remote_copy(
                part(source, start + peer * size, size),
                landed.at[pl.ds(slot + (d - 1) * size, size)],
                sems.at[0, number],
                sems.at[1, number],
                device_id=device(peer),
                device_id_type=MESH,
            )
            copy.start()
            copies.append(copy)
            number += 1
        if depth == 1:
            meanwhile()
        start = start + mine * size
        starts.append((start, size))
        total = part(source, start, size)[...]
        for d in range(1, n):
            copies[d - 1].wait_recv()
            total = total + landed[pl.ds(slot + (d - 1) * size, size)]
        slot += (n - 1) * size
        part(acc, start, size)[...] = total
        source = acc
        sent += copies
    part(gathered, start, size)[...] = total
    for (n, mine, device), (start, size) in reversed(list(zip(levels(), starts))):
        copies = []
        for d in range(1, n):
            peer = lax.rem(mine + d, n)
            copy = pltpu.make_async_remote_copy(
                part(gathered, start, size),
                part(gathered, start, size),
                sems.at[0, number],
                sems.at[1, number],
                device_id=device(peer),
                device_id_type=MESH,
            )
            copy.start()
            copies.append(copy)
            number += 1
        for copy in copies:
            copy.wait_recv()
        sent += copies
    for copy in sent:
        copy.wait_send()


LANES = 128


def remote(source, target, sems, piece, number, device):
    return pltpu.make_async_remote_copy(
        source,
        target,
        sems.at[0, piece, number],
        sems.at[1, piece, number],
        device_id=device,
        device_id_type=MESH,
    )


def fused_kernel(
    factor,
    mask,
    ancestor,
    out,
    gathered,
    turned,
    tiles,
    parts,
    first,
    second,
    sums,
    ended,
    landing,
    term,
    acc,
    landed,
    result,
    loads,
    sems,
    small_sems,
):
    n_rows = lax.axis_size("prow")
    n_cols = lax.axis_size("pcol")
    row = lax.axis_index("prow")
    column = lax.axis_index("pcol")
    count, rows_here, width = factor.shape
    slab = out.shape[1]
    pieces = slab // LANES
    half = count * width // 2
    flip_x = row + 1 - 2 * lax.rem(row, 2)
    flip_y = lax.rem(row + 2, 4)
    flip_both = 3 - row
    x_peer, y_peer = (flip_x, column), (flip_y, column)
    place = column * n_rows + row
    target = (lax.div(place, n_cols), lax.rem(place, n_cols))
    here = row * n_cols + column
    origin = (lax.rem(here, n_rows), lax.div(here, n_rows))
    order = (flip_both, flip_x, flip_y, row)
    buffers = tiles.shape[0]
    upper, lower = pl.ds(0, half), pl.ds(half, half)

    def load(t):
        start = pl.multiple_of(order[t % 4] * slab + (t // 4) * LANES, LANES)
        return pltpu.make_async_copy(ancestor.at[:, pl.ds(start, LANES)], tiles.at[t % buffers], loads.at[t])

    for t in range(buffers):
        load(t).start()

    barrier = pltpu.get_barrier_semaphore()
    peers = [device(lax.rem(mine + d, n)) for n, mine, device in levels() for d in range(1, n)]
    for peer in peers:
        pl.semaphore_signal(barrier, inc=1, device_id=peer, device_id_type=MESH)

    @pl.when(place != here)
    def _():
        pl.semaphore_signal(barrier, inc=1, device_id=origin, device_id_type=MESH)

    for k in range(count):
        for i in range(0, rows_here, WIDTH):
            block = factor[k, pl.ds(i, WIDTH)].T.astype(jnp.float32) * mask[pl.ds(k, 1), pl.ds(i, WIDTH)]
            turned[pl.ds(k * width, width), pl.ds(i, WIDTH)] = block.astype(jnp.bfloat16)

    @pl.when(place != here)
    def _():
        pl.semaphore_wait(barrier, len(peers) + 1)

    @pl.when(place == here)
    def _():
        pl.semaphore_wait(barrier, len(peers))

    def early(j):
        return (
            remote(parts.at[4 * j, upper], first.at[j, 0], sems, j, 0, x_peer),
            remote(parts.at[4 * j + 1, upper], first.at[j, 1], sems, j, 1, x_peer),
            remote(parts.at[4 * j, lower], first.at[j, 2], sems, j, 2, y_peer),
            remote(parts.at[4 * j + 2, lower], first.at[j, 3], sems, j, 3, y_peer),
        )

    def late(j):
        return (
            remote(sums.at[j, 0], second.at[j, 0], sems, j, 4, y_peer),
            remote(sums.at[j, 1], second.at[j, 1], sems, j, 5, x_peer),
        )

    def final(j):
        return remote(ended.at[j], landing.at[j], sems, j, 6, target)

    def compute(j):
        for q in range(4):
            t = 4 * j + q
            load(t).wait()
            value = tiles[t % buffers]
            high = value.astype(jnp.bfloat16)
            low = (value - high.astype(jnp.float32)).astype(jnp.bfloat16)
            both = dot(turned[...], jnp.concatenate([high, low], axis=1))
            parts[t] = both[:, :LANES] + both[:, LANES:]
            if t + buffers < 4 * pieces:
                load(t + buffers).start()
            copies = early(j)
            for i in ((0, 2), (1,), (3,), ())[q]:
                copies[i].start()

    def forward(j):
        copies = early(j)
        copies[0].wait_recv()
        sums[j, 0] = parts[4 * j + 2, upper] + first[j, 0]
        late(j)[0].start()
        copies[2].wait_recv()
        sums[j, 1] = parts[4 * j + 1, lower] + first[j, 2]
        late(j)[1].start()

    def end(j):
        copies = early(j)
        copies[1].wait_recv()
        copies[3].wait_recv()
        late(j)[0].wait_recv()
        late(j)[1].wait_recv()
        ended[j, upper] = parts[4 * j + 3, upper] + first[j, 1] + second[j, 0]
        ended[j, lower] = parts[4 * j + 3, lower] + first[j, 3] + second[j, 1]

        @pl.when(place != here)
        def _():
            final(j).start()

        @pl.when(place == here)
        def _():
            landing[j] = ended[j]

    for j in range(pieces):
        compute(j)
        if j >= 1:
            forward(j - 1)
        if j >= 2:
            end(j - 2)
    forward(pieces - 1)
    for j in range(max(pieces - 2, 0), pieces):
        end(j)
    totals = [0.0] * count
    for j in range(pieces):
        @pl.when(place != here)
        def _():
            final(j).wait_recv()

        lanes = pl.ds(pl.multiple_of(column * slab + j * LANES, LANES), LANES)
        for k in range(count):
            rows = pl.ds(k * width, width)
            value = landing[j, rows]
            high = value.astype(jnp.bfloat16)
            low = (value - high.astype(jnp.float32)).astype(jnp.bfloat16)
            own = turned[rows, lanes]
            totals[k] = totals[k] + lax.dot_general(
                jnp.concatenate([own, own], axis=1),
                jnp.concatenate([high, low], axis=1),
                (((1,), (1,)), ((), ())),
                preferred_element_type=jnp.float32,
            )
    for k in range(count):
        term[pl.ds(k * width, width)] = totals[k]

    def meanwhile():
        for j in range(pieces):
            for k in range(count):
                out[k, pl.ds(j * LANES, LANES)] = landing[j, pl.ds(k * width, width)].T

    sum_everywhere(term, acc, landed, result, small_sems, meanwhile)
    gathered[...] = result[...]
    for j in range(pieces):
        @pl.when(place != here)
        def _():
            final(j).wait_send()

        for copy in early(j) + late(j):
            copy.wait_send()


def fused(factor, mask, ancestor):
    count, depth, width = factor.shape
    height = count * width
    n_rows, n_cols = lax.axis_size("prow"), lax.axis_size("pcol")
    slab = ancestor.shape[1] // n_rows
    pieces = slab // LANES
    half = height // 2
    vmem = pl.BlockSpec(memory_space=pltpu.VMEM)
    f32 = jnp.float32
    block = pltpu.VMEM((height, width), f32)
    small = 2 * (1 + n_rows - 1 + n_cols // 2 - 1)
    return pl.pallas_call(
        fused_kernel,
        out_shape=(
            jax.ShapeDtypeStruct((count, slab, width), f32),
            jax.ShapeDtypeStruct((height, width), f32),
        ),
        in_specs=[vmem, vmem, pl.BlockSpec(memory_space=pl.ANY)],
        out_specs=(vmem, vmem),
        scratch_shapes=[
            pltpu.VMEM((height, depth), jnp.bfloat16),
            pltpu.VMEM((4, depth, LANES), f32),
            pltpu.VMEM((4 * pieces, height, LANES), f32),
            pltpu.VMEM((pieces, 4, half, LANES), f32),
            pltpu.VMEM((pieces, 2, half, LANES), f32),
            pltpu.VMEM((pieces, 2, half, LANES), f32),
            pltpu.VMEM((pieces, height, LANES), f32),
            pltpu.VMEM((pieces, height, LANES), f32),
            block,
            block,
            block,
            block,
            pltpu.SemaphoreType.DMA((4 * pieces,)),
            pltpu.SemaphoreType.DMA((2, pieces, 7)),
            pltpu.SemaphoreType.DMA((2, small)),
        ],
        compiler_params=pltpu.CompilerParams(
            collective_id=1, has_side_effects=True, vmem_limit_bytes=48 * 1024 * 1024
        ),
    )(factor, mask, ancestor)


def product_plain(turned, ancestor):
    n_rows = lax.axis_size("prow")
    n_cols = lax.axis_size("pcol")
    high, low = split(ancestor)
    partial = dot(turned, high) + dot(turned, low)
    summed = lax.psum_scatter(partial, "prow", scatter_dimension=1, tiled=True)
    pairs = [(r * n_cols + c, c * n_rows + r) for r in range(n_rows) for c in range(n_cols)]
    return lax.ppermute(summed, ("prow", "pcol"), pairs)


def shards(ancestor, factor, inverse_diag, block_mask):
    rows_here = ancestor.shape[0]
    count, _, width = factor.shape
    n_rows = lax.axis_size("prow")
    n_cols = lax.axis_size("pcol")
    column = lax.axis_index("pcol")
    grid_row = lax.axis_index("prow")
    slab = rows_here // n_cols
    row_mask = jnp.repeat(block_mask, WIDTH, axis=1).astype(jnp.float32)
    own_mask = lax.dynamic_slice_in_dim(row_mask, grid_row * rows_here, rows_here, 1)
    slab_mask = lax.dynamic_slice_in_dim(own_mask, column * slab, slab, 1)
    inverse = inverse_diag.astype(jnp.float32)
    fits = n_rows == 4 and n_cols % 2 == 0 and count % 2 == 0
    fits = fits and slab % LANES == 0 and count * width % (8 * n_rows * n_cols) == 0
    if fits:
        placed, total = fused(factor, own_mask, ancestor)
        return (-slab_mask[:, :, None] * placed, inverse + total.reshape(inverse.shape))
    masked = factor * own_mask[:, :, None].astype(factor.dtype)
    turned = masked.transpose(0, 2, 1).reshape(count * width, rows_here)
    placed = product_plain(turned, ancestor).reshape(count, width, slab)
    column_block = -slab_mask[:, :, None] * placed.transpose(0, 2, 1)
    own_slab = lax.dynamic_slice_in_dim(masked, column * slab, slab, 1)
    high, low = split(column_block)
    term = jnp.stack([dot(own_slab[k].T, high[k]) + dot(own_slab[k].T, low[k]) for k in range(count)])
    return (column_block, inverse - lax.psum(term, ("prow", "pcol")))


def solution(mesh):
    return jax.shard_map(
        shards,
        mesh=mesh,
        in_specs=(P("prow", "pcol"), P(None, "prow", None), P(), P()),
        out_specs=(P(None, ("prow", "pcol"), None), P()),
        check_vma=False,
    )
```

```python
import jax
import jax.numpy as jnp
from jax import lax
from jax.experimental import pallas as pl
from jax.experimental.pallas import tpu as pltpu
from jax.sharding import PartitionSpec as P

WIDTH = 256


def split(x):
    high = lax.reduce_precision(x, 8, 7)
    low = x - high
    return high.astype(jnp.bfloat16), low.astype(jnp.bfloat16)


def dot(a, b):
    return jnp.dot(a, b, preferred_element_type=jnp.float32)


MESH = pl.DeviceIdType.MESH


def levels():
    n_rows = lax.axis_size("prow")
    n_deep = lax.axis_size("pcol") // 2
    row = lax.axis_index("prow")
    column = lax.axis_index("pcol")
    deep, core = lax.div(column, 2), lax.rem(column, 2)
    return (
        (2, core, lambda p: (row, deep * 2 + p)),
        (n_rows, row, lambda p: (p, column)),
        (n_deep, deep, lambda p: (row, p * 2 + core)),
    )


def part(ref, start, size):
    return ref.at[pl.ds(pl.multiple_of(start, 8), size)]


def sum_everywhere(term, acc, landed, gathered, sems, base, height, number):
    start = base
    size = height
    slot = base
    source = term
    sent = []
    starts = []
    for n, mine, device in levels():
        size = size // n
        copies = []
        for d in range(1, n):
            peer = lax.rem(mine + d, n)
            copy = pltpu.make_async_remote_copy(
                part(source, start + peer * size, size),
                landed.at[pl.ds(slot + (d - 1) * size, size)],
                sems.at[0, number],
                sems.at[1, number],
                device_id=device(peer),
                device_id_type=MESH,
            )
            copy.start()
            copies.append(copy)
            number += 1
        yield
        start = start + mine * size
        starts.append((start, size))
        total = part(source, start, size)[...]
        for d in range(1, n):
            copies[d - 1].wait_recv()
            total = total + landed[pl.ds(slot + (d - 1) * size, size)]
        slot += (n - 1) * size
        part(acc, start, size)[...] = total
        source = acc
        sent += copies
    part(gathered, start, size)[...] = total
    for (n, mine, device), (start, size) in reversed(list(zip(levels(), starts))):
        copies = []
        for d in range(1, n):
            peer = lax.rem(mine + d, n)
            copy = pltpu.make_async_remote_copy(
                part(gathered, start, size),
                part(gathered, start, size),
                sems.at[0, number],
                sems.at[1, number],
                device_id=device(peer),
                device_id_type=MESH,
            )
            copy.start()
            copies.append(copy)
            number += 1
        yield
        for copy in copies:
            copy.wait_recv()
        sent += copies
    for copy in sent:
        copy.wait_send()


def chunk_of(position, deep):
    across = lax.rem(position + deep, 2)
    along = lax.rem(lax.div(position, 2) + lax.div(deep, 2), 2)
    return 2 * lax.rem(across + along, 2) + along


def position_of(chunk, deep):
    along = lax.rem(chunk, 2)
    across = lax.rem(lax.div(chunk, 2) + along, 2)
    return lax.rem(across + deep, 2) + 2 * lax.rem(along + lax.div(deep, 2), 2)


LANES = 128


def remote(source, target, sems, piece, number, device):
    return pltpu.make_async_remote_copy(
        source,
        target,
        sems.at[0, piece, number],
        sems.at[1, piece, number],
        device_id=device,
        device_id_type=MESH,
    )


def fused_kernel(
    factor,
    mask,
    ancestor,
    out,
    gathered,
    turned,
    tiles,
    parts,
    first,
    second,
    sums,
    ended,
    landing,
    term,
    acc,
    landed,
    result,
    loads,
    sems,
    small_sems,
):
    n_rows = lax.axis_size("prow")
    n_cols = lax.axis_size("pcol")
    row = lax.axis_index("prow")
    column = lax.axis_index("pcol")
    count, rows_here, width = factor.shape
    slab = out.shape[1]
    pieces = slab // LANES
    half = count * width // 2
    flip_x = row + 1 - 2 * lax.rem(row, 2)
    flip_y = lax.rem(row + 2, 4)
    flip_both = 3 - row
    x_peer, y_peer = (flip_x, column), (flip_y, column)
    deep = lax.div(column, 2)
    place = column * n_rows + chunk_of(row, deep)
    target = (lax.div(place, n_cols), lax.rem(place, n_cols))
    here = row * n_cols + column
    from_column = lax.div(here, n_rows)
    origin = (position_of(lax.rem(here, n_rows), lax.div(from_column, 2)), from_column)
    order = (flip_both, flip_x, flip_y, row)
    buffers = tiles.shape[0]
    upper, lower = pl.ds(0, half), pl.ds(half, half)

    def load(t):
        start = pl.multiple_of(chunk_of(order[t % 4], deep) * slab + (t // 4) * LANES, LANES)
        return pltpu.make_async_copy(ancestor.at[:, pl.ds(start, LANES)], tiles.at[t % buffers], loads.at[t])

    for t in range(buffers):
        load(t).start()

    barrier = pltpu.get_barrier_semaphore()
    peers = [device(lax.rem(mine + d, n)) for n, mine, device in levels() for d in range(1, n)]
    for peer in peers:
        pl.semaphore_signal(barrier, inc=1, device_id=peer, device_id_type=MESH)

    @pl.when(place != here)
    def _():
        pl.semaphore_signal(barrier, inc=1, device_id=origin, device_id_type=MESH)

    for k in range(count):
        for i in range(0, rows_here, WIDTH):
            block = factor[k, pl.ds(i, WIDTH)].T.astype(jnp.float32) * mask[pl.ds(k, 1), pl.ds(i, WIDTH)]
            turned[pl.ds(k * width, width), pl.ds(i, WIDTH)] = block.astype(jnp.bfloat16)

    @pl.when(place != here)
    def _():
        pl.semaphore_wait(barrier, len(peers) + 1)

    @pl.when(place == here)
    def _():
        pl.semaphore_wait(barrier, len(peers))

    def early(j):
        return (
            remote(parts.at[4 * j, upper], first.at[j, 0], sems, j, 0, x_peer),
            remote(parts.at[4 * j + 1, upper], first.at[j, 1], sems, j, 1, x_peer),
            remote(parts.at[4 * j, lower], first.at[j, 2], sems, j, 2, y_peer),
            remote(parts.at[4 * j + 2, lower], first.at[j, 3], sems, j, 3, y_peer),
        )

    def late(j):
        return (
            remote(sums.at[j, 0], second.at[j, 0], sems, j, 4, y_peer),
            remote(sums.at[j, 1], second.at[j, 1], sems, j, 5, x_peer),
        )

    def final(j):
        return remote(ended.at[j], landing.at[j], sems, j, 6, target)

    def compute(j):
        for q in range(4):
            t = 4 * j + q
            load(t).wait()
            value = tiles[t % buffers]
            high = value.astype(jnp.bfloat16)
            low = (value - high.astype(jnp.float32)).astype(jnp.bfloat16)
            both = dot(turned[...], jnp.concatenate([high, low], axis=1))
            parts[t] = both[:, :LANES] + both[:, LANES:]
            if t + buffers < 4 * pieces:
                load(t + buffers).start()
            copies = early(j)
            for i in ((0, 2), (1,), (3,), ())[q]:
                copies[i].start()

    def forward(j):
        copies = early(j)
        copies[0].wait_recv()
        sums[j, 0] = parts[4 * j + 2, upper] + first[j, 0]
        late(j)[0].start()
        copies[2].wait_recv()
        sums[j, 1] = parts[4 * j + 1, lower] + first[j, 2]
        late(j)[1].start()

    def end(j):
        copies = early(j)
        copies[1].wait_recv()
        copies[3].wait_recv()
        late(j)[0].wait_recv()
        late(j)[1].wait_recv()
        ended[j, upper] = parts[4 * j + 3, upper] + first[j, 1] + second[j, 0]
        ended[j, lower] = parts[4 * j + 3, lower] + first[j, 3] + second[j, 1]

        @pl.when(place != here)
        def _():
            final(j).start()

        @pl.when(place == here)
        def _():
            landing[j] = ended[j]

    for j in range(pieces):
        compute(j)
        if j >= 1:
            forward(j - 1)
        if j >= 2:
            end(j - 2)
    forward(pieces - 1)
    for j in range(max(pieces - 2, 0), pieces):
        end(j)
    totals = [0.0] * count
    for j in range(pieces):
        @pl.when(place != here)
        def _():
            final(j).wait_recv()

        lanes = pl.ds(pl.multiple_of(column * slab + j * LANES, LANES), LANES)
        for k in range(count):
            rows = pl.ds(k * width, width)
            value = landing[j, rows]
            high = value.astype(jnp.bfloat16)
            low = (value - high.astype(jnp.float32)).astype(jnp.bfloat16)
            own = turned[rows, lanes]
            totals[k] = totals[k] + lax.dot_general(
                jnp.concatenate([own, own], axis=1),
                jnp.concatenate([high, low], axis=1),
                (((1,), (1,)), ((), ())),
                preferred_element_type=jnp.float32,
            )
    for k in range(count):
        term[pl.ds(k * width, width)] = totals[k]

    def meanwhile():
        for j in range(pieces):
            for k in range(count):
                out[k, pl.ds(j * LANES, LANES)] = landing[j, pl.ds(k * width, width)].T

    each = small_sems.shape[1] // 2
    halves = [
        sum_everywhere(term, acc, landed, result, small_sems, h * half, half, h * each) for h in range(2)
    ]
    for depth in range(7):
        for running in halves:
            next(running, None)
        if depth == 1:
            meanwhile()
    gathered[...] = result[...]
    for j in range(pieces):
        @pl.when(place != here)
        def _():
            final(j).wait_send()

        for copy in early(j) + late(j):
            copy.wait_send()


def fused(factor, mask, ancestor):
    count, depth, width = factor.shape
    height = count * width
    n_rows, n_cols = lax.axis_size("prow"), lax.axis_size("pcol")
    slab = ancestor.shape[1] // n_rows
    pieces = slab // LANES
    half = height // 2
    vmem = pl.BlockSpec(memory_space=pltpu.VMEM)
    f32 = jnp.float32
    block = pltpu.VMEM((height, width), f32)
    small = 4 * (1 + n_rows - 1 + n_cols // 2 - 1)
    return pl.pallas_call(
        fused_kernel,
        out_shape=(
            jax.ShapeDtypeStruct((count, slab, width), f32),
            jax.ShapeDtypeStruct((height, width), f32),
        ),
        in_specs=[vmem, vmem, pl.BlockSpec(memory_space=pl.ANY)],
        out_specs=(vmem, vmem),
        scratch_shapes=[
            pltpu.VMEM((height, depth), jnp.bfloat16),
            pltpu.VMEM((4, depth, LANES), f32),
            pltpu.VMEM((4 * pieces, height, LANES), f32),
            pltpu.VMEM((pieces, 4, half, LANES), f32),
            pltpu.VMEM((pieces, 2, half, LANES), f32),
            pltpu.VMEM((pieces, 2, half, LANES), f32),
            pltpu.VMEM((pieces, height, LANES), f32),
            pltpu.VMEM((pieces, height, LANES), f32),
            block,
            block,
            block,
            block,
            pltpu.SemaphoreType.DMA((4 * pieces,)),
            pltpu.SemaphoreType.DMA((2, pieces, 7)),
            pltpu.SemaphoreType.DMA((2, small)),
        ],
        compiler_params=pltpu.CompilerParams(
            collective_id=1, has_side_effects=True, vmem_limit_bytes=48 * 1024 * 1024
        ),
    )(factor, mask, ancestor)


def product_plain(turned, ancestor):
    n_rows = lax.axis_size("prow")
    n_cols = lax.axis_size("pcol")
    high, low = split(ancestor)
    partial = dot(turned, high) + dot(turned, low)
    summed = lax.psum_scatter(partial, "prow", scatter_dimension=1, tiled=True)
    pairs = [(r * n_cols + c, c * n_rows + r) for r in range(n_rows) for c in range(n_cols)]
    return lax.ppermute(summed, ("prow", "pcol"), pairs)


def shards(ancestor, factor, inverse_diag, block_mask):
    rows_here = ancestor.shape[0]
    count, _, width = factor.shape
    n_rows = lax.axis_size("prow")
    n_cols = lax.axis_size("pcol")
    column = lax.axis_index("pcol")
    grid_row = lax.axis_index("prow")
    slab = rows_here // n_cols
    row_mask = jnp.repeat(block_mask, WIDTH, axis=1).astype(jnp.float32)
    own_mask = lax.dynamic_slice_in_dim(row_mask, grid_row * rows_here, rows_here, 1)
    slab_mask = lax.dynamic_slice_in_dim(own_mask, column * slab, slab, 1)
    inverse = inverse_diag.astype(jnp.float32)
    fits = n_rows == 4 and n_cols % 2 == 0 and count % 2 == 0
    fits = fits and slab % LANES == 0 and count * width % (16 * n_rows * n_cols) == 0
    if fits:
        placed, total = fused(factor, own_mask, ancestor)
        return (-slab_mask[:, :, None] * placed, inverse + total.reshape(inverse.shape))
    masked = factor * own_mask[:, :, None].astype(factor.dtype)
    turned = masked.transpose(0, 2, 1).reshape(count * width, rows_here)
    placed = product_plain(turned, ancestor).reshape(count, width, slab)
    column_block = -slab_mask[:, :, None] * placed.transpose(0, 2, 1)
    own_slab = lax.dynamic_slice_in_dim(masked, column * slab, slab, 1)
    high, low = split(column_block)
    term = jnp.stack([dot(own_slab[k].T, high[k]) + dot(own_slab[k].T, low[k]) for k in range(count)])
    return (column_block, inverse - lax.psum(term, ("prow", "pcol")))


def solution(mesh):
    return jax.shard_map(
        shards,
        mesh=mesh,
        in_specs=(P("prow", "pcol"), P(None, "prow", None), P(), P()),
        out_specs=(P(None, ("prow", "pcol"), None), P()),
        check_vma=False,
    )
```

```python
import jax
import jax.numpy as jnp
from jax import lax
from jax.experimental import pallas as pl
from jax.experimental.pallas import tpu as pltpu
from jax.sharding import PartitionSpec as P

WIDTH = 256


def split(x):
    high = lax.reduce_precision(x, 8, 7)
    low = x - high
    return high.astype(jnp.bfloat16), low.astype(jnp.bfloat16)


def dot(a, b):
    return jnp.dot(a, b, preferred_element_type=jnp.float32)


MESH = pl.DeviceIdType.MESH


def levels():
    n_rows = lax.axis_size("prow")
    n_deep = lax.axis_size("pcol") // 2
    row = lax.axis_index("prow")
    column = lax.axis_index("pcol")
    deep, core = lax.div(column, 2), lax.rem(column, 2)
    return (
        (2, core, lambda p: (row, deep * 2 + p)),
        (n_rows, row, lambda p: (p, column)),
        (n_deep, deep, lambda p: (row, p * 2 + core)),
    )


def part(ref, start, size):
    return ref.at[pl.ds(pl.multiple_of(start, 8), size)]


def sum_everywhere(term, acc, landed, gathered, sems, base, height, number):
    start = base
    size = height
    slot = base
    source = term
    sent = []
    starts = []
    for n, mine, device in levels():
        size = size // n
        copies = []
        for d in range(1, n):
            peer = lax.rem(mine + d, n)
            copy = pltpu.make_async_remote_copy(
                part(source, start + peer * size, size),
                landed.at[pl.ds(slot + (d - 1) * size, size)],
                sems.at[0, number],
                sems.at[1, number],
                device_id=device(peer),
                device_id_type=MESH,
            )
            copy.start()
            copies.append(copy)
            number += 1
        yield
        start = start + mine * size
        starts.append((start, size))
        total = part(source, start, size)[...]
        for d in range(1, n):
            copies[d - 1].wait_recv()
            total = total + landed[pl.ds(slot + (d - 1) * size, size)]
        slot += (n - 1) * size
        part(acc, start, size)[...] = total
        source = acc
        sent += copies
    part(gathered, start, size)[...] = total
    for (n, mine, device), (start, size) in reversed(list(zip(levels(), starts))):
        copies = []
        for d in range(1, n):
            peer = lax.rem(mine + d, n)
            copy = pltpu.make_async_remote_copy(
                part(gathered, start, size),
                part(gathered, start, size),
                sems.at[0, number],
                sems.at[1, number],
                device_id=device(peer),
                device_id_type=MESH,
            )
            copy.start()
            copies.append(copy)
            number += 1
        yield
        for copy in copies:
            copy.wait_recv()
        sent += copies
    for copy in sent:
        copy.wait_send()


def chunk_of(position, deep):
    across = lax.rem(position + deep, 2)
    along = lax.rem(lax.div(position, 2) + lax.div(deep, 2), 2)
    return 2 * lax.rem(across + along, 2) + along


def position_of(chunk, deep):
    along = lax.rem(chunk, 2)
    across = lax.rem(lax.div(chunk, 2) + along, 2)
    return lax.rem(across + deep, 2) + 2 * lax.rem(along + lax.div(deep, 2), 2)


LANES = 128


def remote(source, target, sems, piece, number, device):
    return pltpu.make_async_remote_copy(
        source,
        target,
        sems.at[0, piece, number],
        sems.at[1, piece, number],
        device_id=device,
        device_id_type=MESH,
    )


def fused_kernel(
    factor,
    mask,
    ancestor,
    out,
    gathered,
    turned,
    tiles,
    parts,
    first,
    second,
    sums,
    ended,
    landing,
    term,
    acc,
    landed,
    result,
    loads,
    sems,
    small_sems,
):
    n_rows = lax.axis_size("prow")
    n_cols = lax.axis_size("pcol")
    row = lax.axis_index("prow")
    column = lax.axis_index("pcol")
    count, rows_here, width = factor.shape
    slab = out.shape[1]
    pieces = slab // LANES
    half = count * width // 2
    flip_x = row + 1 - 2 * lax.rem(row, 2)
    flip_y = lax.rem(row + 2, 4)
    flip_both = 3 - row
    x_peer, y_peer = (flip_x, column), (flip_y, column)
    deep = lax.div(column, 2)
    place = column * n_rows + chunk_of(row, deep)
    target = (lax.div(place, n_cols), lax.rem(place, n_cols))
    here = row * n_cols + column
    from_column = lax.div(here, n_rows)
    origin = (position_of(lax.rem(here, n_rows), lax.div(from_column, 2)), from_column)
    order = (flip_both, flip_x, flip_y, row)
    buffers = tiles.shape[0]
    upper, lower = pl.ds(0, half), pl.ds(half, half)

    def load(t):
        start = pl.multiple_of(chunk_of(order[t % 4], deep) * slab + (t // 4) * LANES, LANES)
        return pltpu.make_async_copy(ancestor.at[:, pl.ds(start, LANES)], tiles.at[t % buffers], loads.at[t])

    for t in range(buffers):
        load(t).start()

    barrier = pltpu.get_barrier_semaphore()
    peers = [device(lax.rem(mine + d, n)) for n, mine, device in levels() for d in range(1, n)]
    for peer in peers:
        pl.semaphore_signal(barrier, inc=1, device_id=peer, device_id_type=MESH)

    @pl.when(place != here)
    def _():
        pl.semaphore_signal(barrier, inc=1, device_id=origin, device_id_type=MESH)

    for k in range(count):
        for i in range(0, rows_here, WIDTH):
            block = factor[k, pl.ds(i, WIDTH)].T.astype(jnp.float32) * mask[pl.ds(k, 1), pl.ds(i, WIDTH)]
            turned[pl.ds(k * width, width), pl.ds(i, WIDTH)] = block.astype(jnp.bfloat16)

    @pl.when(place != here)
    def _():
        pl.semaphore_wait(barrier, len(peers) + 1)

    @pl.when(place == here)
    def _():
        pl.semaphore_wait(barrier, len(peers))

    def early(j):
        return (
            remote(parts.at[4 * j, upper], first.at[j, 0], sems, j, 0, x_peer),
            remote(parts.at[4 * j + 1, upper], first.at[j, 1], sems, j, 1, x_peer),
            remote(parts.at[4 * j, lower], first.at[j, 2], sems, j, 2, y_peer),
            remote(parts.at[4 * j + 2, lower], first.at[j, 3], sems, j, 3, y_peer),
        )

    def late(j):
        return (
            remote(sums.at[j, 0], second.at[j, 0], sems, j, 4, y_peer),
            remote(sums.at[j, 1], second.at[j, 1], sems, j, 5, x_peer),
        )

    def final(j):
        return remote(ended.at[j], landing.at[j], sems, j, 6, target)

    def compute(j):
        for q in range(4):
            t = 4 * j + q
            load(t).wait()
            value = tiles[t % buffers]
            high = value.astype(jnp.bfloat16)
            low = (value - high.astype(jnp.float32)).astype(jnp.bfloat16)
            both = dot(turned[...], jnp.concatenate([high, low], axis=1))
            parts[t] = both[:, :LANES] + both[:, LANES:]
            if t + buffers < 4 * pieces:
                load(t + buffers).start()
            copies = early(j)
            for i in ((0, 2), (1,), (3,), ())[q]:
                copies[i].start()
            if j >= 1 and q == 1:
                forward(j - 1)

    def forward(j):
        copies = early(j)
        copies[0].wait_recv()
        sums[j, 0] = parts[4 * j + 2, upper] + first[j, 0]
        late(j)[0].start()
        copies[2].wait_recv()
        sums[j, 1] = parts[4 * j + 1, lower] + first[j, 2]
        late(j)[1].start()

    def end(j):
        copies = early(j)
        copies[1].wait_recv()
        copies[3].wait_recv()
        late(j)[0].wait_recv()
        late(j)[1].wait_recv()
        ended[j, upper] = parts[4 * j + 3, upper] + first[j, 1] + second[j, 0]
        ended[j, lower] = parts[4 * j + 3, lower] + first[j, 3] + second[j, 1]

        @pl.when(place != here)
        def _():
            final(j).start()

        @pl.when(place == here)
        def _():
            landing[j] = ended[j]

    for j in range(pieces):
        compute(j)
        if j >= 1:
            end(j - 1)
    forward(pieces - 1)
    end(pieces - 1)
    totals = [0.0] * count
    for j in range(pieces):
        @pl.when(place != here)
        def _():
            final(j).wait_recv()

        lanes = pl.ds(pl.multiple_of(column * slab + j * LANES, LANES), LANES)
        for k in range(count):
            rows = pl.ds(k * width, width)
            value = landing[j, rows]
            high = value.astype(jnp.bfloat16)
            low = (value - high.astype(jnp.float32)).astype(jnp.bfloat16)
            own = turned[rows, lanes]
            totals[k] = totals[k] + lax.dot_general(
                jnp.concatenate([own, own], axis=1),
                jnp.concatenate([high, low], axis=1),
                (((1,), (1,)), ((), ())),
                preferred_element_type=jnp.float32,
            )
    for k in range(count):
        term[pl.ds(k * width, width)] = totals[k]

    def meanwhile():
        for j in range(pieces):
            for k in range(count):
                out[k, pl.ds(j * LANES, LANES)] = landing[j, pl.ds(k * width, width)].T

    each = small_sems.shape[1] // 2
    halves = [
        sum_everywhere(term, acc, landed, result, small_sems, h * half, half, h * each) for h in range(2)
    ]
    for depth in range(7):
        for running in halves:
            next(running, None)
        if depth == 1:
            meanwhile()
    gathered[...] = result[...]
    for j in range(pieces):
        @pl.when(place != here)
        def _():
            final(j).wait_send()

        for copy in early(j) + late(j):
            copy.wait_send()


def fused(factor, mask, ancestor):
    count, depth, width = factor.shape
    height = count * width
    n_rows, n_cols = lax.axis_size("prow"), lax.axis_size("pcol")
    slab = ancestor.shape[1] // n_rows
    pieces = slab // LANES
    half = height // 2
    vmem = pl.BlockSpec(memory_space=pltpu.VMEM)
    f32 = jnp.float32
    block = pltpu.VMEM((height, width), f32)
    small = 4 * (1 + n_rows - 1 + n_cols // 2 - 1)
    return pl.pallas_call(
        fused_kernel,
        out_shape=(
            jax.ShapeDtypeStruct((count, slab, width), f32),
            jax.ShapeDtypeStruct((height, width), f32),
        ),
        in_specs=[vmem, vmem, pl.BlockSpec(memory_space=pl.ANY)],
        out_specs=(vmem, vmem),
        scratch_shapes=[
            pltpu.VMEM((height, depth), jnp.bfloat16),
            pltpu.VMEM((4, depth, LANES), f32),
            pltpu.VMEM((4 * pieces, height, LANES), f32),
            pltpu.VMEM((pieces, 4, half, LANES), f32),
            pltpu.VMEM((pieces, 2, half, LANES), f32),
            pltpu.VMEM((pieces, 2, half, LANES), f32),
            pltpu.VMEM((pieces, height, LANES), f32),
            pltpu.VMEM((pieces, height, LANES), f32),
            block,
            block,
            block,
            block,
            pltpu.SemaphoreType.DMA((4 * pieces,)),
            pltpu.SemaphoreType.DMA((2, pieces, 7)),
            pltpu.SemaphoreType.DMA((2, small)),
        ],
        compiler_params=pltpu.CompilerParams(
            collective_id=1, has_side_effects=True, vmem_limit_bytes=48 * 1024 * 1024
        ),
    )(factor, mask, ancestor)


def product_plain(turned, ancestor):
    n_rows = lax.axis_size("prow")
    n_cols = lax.axis_size("pcol")
    high, low = split(ancestor)
    partial = dot(turned, high) + dot(turned, low)
    summed = lax.psum_scatter(partial, "prow", scatter_dimension=1, tiled=True)
    pairs = [(r * n_cols + c, c * n_rows + r) for r in range(n_rows) for c in range(n_cols)]
    return lax.ppermute(summed, ("prow", "pcol"), pairs)


def shards(ancestor, factor, inverse_diag, block_mask):
    rows_here = ancestor.shape[0]
    count, _, width = factor.shape
    n_rows = lax.axis_size("prow")
    n_cols = lax.axis_size("pcol")
    column = lax.axis_index("pcol")
    grid_row = lax.axis_index("prow")
    slab = rows_here // n_cols
    row_mask = jnp.repeat(block_mask, WIDTH, axis=1).astype(jnp.float32)
    own_mask = lax.dynamic_slice_in_dim(row_mask, grid_row * rows_here, rows_here, 1)
    slab_mask = lax.dynamic_slice_in_dim(own_mask, column * slab, slab, 1)
    inverse = inverse_diag.astype(jnp.float32)
    fits = n_rows == 4 and n_cols % 2 == 0 and count % 2 == 0
    fits = fits and slab % LANES == 0 and count * width % (16 * n_rows * n_cols) == 0
    if fits:
        placed, total = fused(factor, own_mask, ancestor)
        return (-slab_mask[:, :, None] * placed, inverse + total.reshape(inverse.shape))
    masked = factor * own_mask[:, :, None].astype(factor.dtype)
    turned = masked.transpose(0, 2, 1).reshape(count * width, rows_here)
    placed = product_plain(turned, ancestor).reshape(count, width, slab)
    column_block = -slab_mask[:, :, None] * placed.transpose(0, 2, 1)
    own_slab = lax.dynamic_slice_in_dim(masked, column * slab, slab, 1)
    high, low = split(column_block)
    term = jnp.stack([dot(own_slab[k].T, high[k]) + dot(own_slab[k].T, low[k]) for k in range(count)])
    return (column_block, inverse - lax.psum(term, ("prow", "pcol")))


def solution(mesh):
    return jax.shard_map(
        shards,
        mesh=mesh,
        in_specs=(P("prow", "pcol"), P(None, "prow", None), P(), P()),
        out_specs=(P(None, ("prow", "pcol"), None), P()),
        check_vma=False,
    )
```
